32 devices in a mesh: prow: 8 (over z, y), pcol: 4 (over x, core).
Axes of the slice: x: 2, y: 2, z: 4, core: 2. Of those that a mesh axis runs over, the one named last changes fastest.
Arguments:
- inverse_tiles: bfloat16 [24576, 24576], P('prow', 'pcol'), may hold values from -6 to 6
- panel_blocks: bfloat16 [24576, 1536], P(('prow', 'pcol')), may hold values from -0.0546875 to 0.0546875
- pivot_inverse: bfloat16 [3, 512, 512], replicated, may hold values from -0.25 to 0.25
- diagonal_inverse: float32 [3, 512, 512], replicated, may hold values from -6 to 6
- ancestors: int32 [3, 24], replicated, may hold values from 0 to 47, all different within a row
Outputs:
- cross_blocks: float32 [24576, 1536], P(('prow', 'pcol'))
- diagonal_blocks: float32 [3, 512, 512], replicated
The draws below stay inside these ranges and needn't reach their ends.
Inputs may be any that keep to these rules, and one draw needn't show every extreme that they name: `ancestors`: each row names 24 different blocks, and every block is named by some row.
All inputs are finite; a program needn't handle non-finite values.
Results may differ from the reference program's by a relative error of at most 0.003.
Values may be sent and summed in bfloat16 or wider, within the bound.
A program may use at most 128 MiB of HBM per device.

```python
import jax
import jax.numpy as jnp
from jax import lax

WIDTH = 512
BLOCKS = 48
LISTED = 24
SUPERNODES = 3
ORDER = 24576


def shard_levels(rng, extent, shards, smallest, high):
    loudness = 1.0
    for axis_at, blocks in shards:
        draws = jax.random.uniform(jax.random.fold_in(jax.random.fold_in(rng, 6), axis_at), (blocks,), jnp.float32, smallest / len(shards), high / len(shards))
        loudness = loudness * jnp.repeat(jnp.exp(draws), extent[axis_at] // blocks).reshape((-1,) + (1,) * (len(extent) - 1 - axis_at))
    return loudness


def distinct(rng, rows, count, top, lift):
    sequence = jax.random.permutation(jax.random.fold_in(rng, 1), count)
    pull = sequence
    for power in range(3):
        pull = pull * pull // count
    pull = pull * lift // count
    chance = jax.random.randint(jax.random.fold_in(rng, 2), (rows, count), 0, 4096) + pull
    sure = jax.random.permutation(jax.random.fold_in(rng, 3), rows)[jnp.arange(count) % rows]
    chance = jnp.where(jnp.arange(rows)[:, None] == sure[None, :], 1 << 14, chance)
    score = chance * count + jnp.arange(count)
    return lax.top_k(score.astype(jnp.int32), top)[1].astype(jnp.int32)


def centred(own_key, extent, width, most, shards=(), kind=jnp.bfloat16):
    array = jax.random.normal(own_key, extent, jnp.float32) * width
    if len(shards) > 0:
        array = shard_levels(own_key, extent, shards, -0.22, 0.18) * array
    return jnp.clip(array, min=-most, max=most).astype(kind)


def setup_inputs(seed: int = 0) -> dict:
    keys = jax.random.split(jax.random.key(seed), 6)
    inverse_tiles = centred(keys[0], (ORDER, ORDER), 1.0, 6.0, ((0, 8), (1, 4)))
    panel_blocks = centred(keys[1], (ORDER, SUPERNODES * WIDTH), (LISTED * WIDTH) ** -0.5, 0.0546875, ((0, 32),))
    pivot_inverse = centred(keys[2], (SUPERNODES, WIDTH, WIDTH), WIDTH ** -0.5, 0.25)
    diagonal_inverse = centred(keys[3], (SUPERNODES, WIDTH, WIDTH), 1.0, 6.0, (), jnp.float32)
    ancestors = distinct(keys[4], SUPERNODES, BLOCKS, LISTED, 4096)
    return {"inverse_tiles": inverse_tiles, "panel_blocks": panel_blocks, "pivot_inverse": pivot_inverse, "diagonal_inverse": diagonal_inverse, "ancestors": ancestors}


def reference(inverse_tiles, panel_blocks, pivot_inverse, diagonal_inverse, ancestors):
    rows_all = BLOCKS * WIDTH
    member = jnp.any(ancestors[:, :, None] == jnp.arange(BLOCKS, dtype=jnp.int32)[None, None, :], axis=1).astype(jnp.float32)
    listed = jnp.repeat(member.T, WIDTH, axis=0)
    raw_three = panel_blocks.reshape(rows_all, SUPERNODES, WIDTH).astype(jnp.float32)
    normed = jnp.einsum("rsw,swv->rsv", raw_three, pivot_inverse.astype(jnp.float32), precision=lax.Precision.HIGHEST)
    scaled = (normed * listed[:, :, None]).astype(jnp.bfloat16)
    panel = scaled.reshape(rows_all, SUPERNODES * WIDTH)

    def one_block(tile_rows):
        return jnp.dot(tile_rows, panel, preferred_element_type=jnp.float32)

    product = lax.map(one_block, inverse_tiles.reshape(BLOCKS, WIDTH, rows_all))
    product = product.reshape(rows_all, SUPERNODES, WIDTH)
    cross = -(product * listed[:, :, None])
    terms = jnp.einsum("rsw,rsv->swv", scaled.astype(jnp.float32), cross, precision=lax.Precision.HIGHEST)
    diagonal = diagonal_inverse - terms
    return cross.reshape(rows_all, SUPERNODES * WIDTH), diagonal
```

```python
import jax
import jax.numpy as jnp
from jax import lax
from jax.sharding import PartitionSpec as P


def reduce_rows(partial, seg_rows):
    devices = lax.axis_size("pcol")
    width = partial.shape[1]
    me = lax.axis_index("pcol")
    if devices & (devices - 1):
        return lax.psum_scatter(partial, "pcol", scatter_dimension=0, tiled=True)
    value = partial.reshape(devices, seg_rows, width)
    bit = 1
    while bit < devices:
        mine = (me // bit) % 2
        halves = value.reshape(value.shape[0] // 2, 2, seg_rows, width)
        keep = jnp.where(mine == 0, halves[:, 0], halves[:, 1])
        send = jnp.where(mine == 0, halves[:, 1], halves[:, 0]).astype(jnp.bfloat16)
        got = lax.ppermute(send, "pcol", [(d, d ^ bit) for d in range(devices)])
        value = keep + got.astype(jnp.float32)
        bit *= 2
    return value.reshape(seg_rows, width)


def on_device(inverse_tiles, panel_blocks, pivot_inverse, diagonal_inverse, ancestors):
    seg_rows = panel_blocks.shape[0]
    n_super = pivot_inverse.shape[0]
    width = pivot_inverse.shape[1]
    row_devices = lax.axis_size("prow")
    col_devices = lax.axis_size("pcol")
    segment = lax.axis_index("prow") * col_devices + lax.axis_index("pcol")
    row_ids = segment * seg_rows + lax.iota(jnp.int32, seg_rows)
    block_ids = row_ids // width
    listed = jnp.any(block_ids[:, None, None] == ancestors[None, :, :], axis=2).astype(jnp.float32)
    route = []
    for s in range(row_devices * col_devices):
        route.append((s, (s % row_devices) * col_devices + s // row_devices))
    crosses, terms = [], []
    scaled, panels = [], []
    for k in range(n_super):
        normed = jnp.dot(
            panel_blocks[:, k * width:(k + 1) * width], pivot_inverse[k],
            preferred_element_type=jnp.float32,
        )
        own = (normed * listed[:, k:k + 1]).astype(jnp.bfloat16)
        scaled.append(own)
        moved = lax.ppermute(own, ("prow", "pcol"), route)
        panels.append(lax.all_gather(moved, "prow", axis=0, tiled=True))
    for k in range(n_super):
        product = jnp.dot(inverse_tiles, panels[k], preferred_element_type=jnp.float32)
        summed = reduce_rows(product, seg_rows)
        cross = -(summed * listed[:, k:k + 1])
        crosses.append(cross)
        term = lax.dot_general(
            scaled[k].astype(jnp.float32), cross, (((0,), (0,)), ((), ())),
            precision=lax.Precision.HIGHEST,
        )
        if terms:
            term, terms[-1] = lax.optimization_barrier((term, terms[-1]))
        terms.append(lax.psum(term, ("prow", "pcol")))
    diagonal = diagonal_inverse - jnp.stack(terms)
    return (jnp.concatenate(crosses, axis=1), diagonal)


def solution(mesh):
    in_specs = (P("prow", "pcol"), P(("prow", "pcol"), None), P(), P(), P())
    out_specs = (P(("prow", "pcol"), None), P())
    return jax.shard_map(
        on_device, mesh=mesh, in_specs=in_specs, out_specs=out_specs, check_vma=False
    )
```

```python
import jax
import jax.numpy as jnp
from jax import lax
from jax.sharding import PartitionSpec as P


def reduce_rows(partial, seg_rows):
    devices = lax.axis_size("pcol")
    width = partial.shape[1]
    me = lax.axis_index("pcol")
    if devices & (devices - 1):
        return lax.psum_scatter(partial, "pcol", scatter_dimension=0, tiled=True)
    value = partial.reshape(devices, seg_rows, width)
    bit = 1
    while bit < devices:
        mine = (me // bit) % 2
        halves = value.reshape(value.shape[0] // 2, 2, seg_rows, width)
        keep = jnp.where(mine == 0, halves[:, 0], halves[:, 1])
        send = jnp.where(mine == 0, halves[:, 1], halves[:, 0]).astype(jnp.bfloat16)
        got = lax.ppermute(send, "pcol", [(d, d ^ bit) for d in range(devices)])
        value = keep + got.astype(jnp.float32)
        bit *= 2
    return value.reshape(seg_rows, width)


def sum_everywhere(terms):
    axes = ("prow", "pcol")
    devices = lax.axis_size("prow") * lax.axis_size("pcol")
    rows = terms.shape[0] * terms.shape[1]
    if devices & (devices - 1) or rows % devices:
        return lax.psum(terms, axes)
    me = lax.axis_index("prow") * lax.axis_size("pcol") + lax.axis_index("pcol")
    value = terms.reshape(rows, terms.shape[2])
    bits = []
    bit = 1
    while bit < devices:
        bits.append(bit)
        bit *= 2
    for bit in bits:
        low = (me // bit) % 2 == 0
        half = value.shape[0] // 2
        keep = jnp.where(low, value[:half], value[half:])
        send = jnp.where(low, value[half:], value[:half])
        value = keep + lax.ppermute(send, axes, [(d, d ^ bit) for d in range(devices)])
    value = value.astype(jnp.bfloat16)
    for bit in reversed(bits):
        low = (me // bit) % 2 == 0
        got = lax.ppermute(value, axes, [(d, d ^ bit) for d in range(devices)])
        value = jnp.concatenate(
            [jnp.where(low, value, got), jnp.where(low, got, value)], axis=0
        )
    return value.astype(jnp.float32).reshape(terms.shape)


def on_device(inverse_tiles, panel_blocks, pivot_inverse, diagonal_inverse, ancestors):
    seg_rows = panel_blocks.shape[0]
    n_super = pivot_inverse.shape[0]
    width = pivot_inverse.shape[1]
    row_devices = lax.axis_size("prow")
    col_devices = lax.axis_size("pcol")
    segment = lax.axis_index("prow") * col_devices + lax.axis_index("pcol")
    row_ids = segment * seg_rows + lax.iota(jnp.int32, seg_rows)
    block_ids = row_ids // width
    listed = jnp.any(block_ids[:, None, None] == ancestors[None, :, :], axis=2).astype(jnp.float32)
    route = []
    for s in range(row_devices * col_devices):
        route.append((s, (s % row_devices) * col_devices + s // row_devices))
    crosses, terms = [], []
    scaled, panels = [], []
    for k in range(n_super):
        normed = jnp.dot(
            panel_blocks[:, k * width:(k + 1) * width], pivot_inverse[k],
            preferred_element_type=jnp.float32,
        )
        own = (normed * listed[:, k:k + 1]).astype(jnp.bfloat16)
        scaled.append(own)
        if k == 0:
            whole = lax.all_gather(own, ("prow", "pcol"), axis=0, tiled=True)
            rows = inverse_tiles.shape[1]
            panels.append(lax.dynamic_slice_in_dim(whole, lax.axis_index("pcol") * rows, rows, 0))
            continue
        if k > 1:
            own, _ = lax.optimization_barrier((own, moved))
        moved = lax.ppermute(own, ("prow", "pcol"), route)
        panels.append(lax.all_gather(moved, "prow", axis=0, tiled=True))
    for k in range(n_super):
        panel = panels[k]
        if k:
            panel, terms[-1] = lax.optimization_barrier((panel, terms[-1]))
        product = jnp.dot(inverse_tiles, panel, preferred_element_type=jnp.float32)
        summed = reduce_rows(product, seg_rows)
        cross = -(summed * listed[:, k:k + 1])
        crosses.append(cross)
        term = lax.dot_general(
            scaled[k].astype(jnp.float32), cross, (((0,), (0,)), ((), ())),
            precision=lax.Precision.HIGHEST,
        )
        terms.append(term)
    diagonal = diagonal_inverse - sum_everywhere(jnp.stack(terms))
    return (jnp.concatenate(crosses, axis=1), diagonal)


def solution(mesh):
    in_specs = (P("prow", "pcol"), P(("prow", "pcol"), None), P(), P(), P())
    out_specs = (P(("prow", "pcol"), None), P())
    return jax.shard_map(
        on_device, mesh=mesh, in_specs=in_specs, out_specs=out_specs, check_vma=False
    )
```
